32 devices in a mesh: frames: 4 (over x, core), feat: 8 (over z, y).
Axes of the slice: x: 2, y: 2, z: 4, core: 2. Of those that a mesh axis runs over, the one named last changes fastest.
Arguments:
- acoustic: float32 [1024, 440], P('frames'), may hold values from -6 to 6
- projection: float32 [440, 8192], P(None, 'feat'), may hold values from -0.25 to 0.25
- phases: float32 [8192], P('feat'), may hold values from -3.140625 to 3.140625
- labels: int32 [1024], P('frames'), may hold values from 0 to 146
- weights: float32 [147, 8192], P(None, 'feat'), may hold values from -1.5 to 1.5
- scaled_duals: float32 [147, 1024], P(None, 'frames'), may hold values from -7 to 7
Outputs:
- weights_out: float32 [147, 8192], P(None, 'feat')
- duals_out: float32 [147, 1024], P(None, ('frames', 'feat'))
- penalty: float32 [], replicated
The draws below stay inside these ranges and needn't reach their ends.
All inputs are finite; a program needn't handle non-finite values.
Results may differ from the reference program's by a relative error of at most 0.0003.
Values sent between devices are 32-bit elements; how exact they have to be, the bound alone decides.
No kernel may reach another device: no remote copies, remote signals or barrier semaphores. Data moves between devices by JAX's collectives and lax.ppermute only.
A program may use at most 64 MiB of HBM per device.

```python
import jax
import jax.numpy as jnp
from jax import lax

DIN = 440
C = 147
FB = 1024
FR_DEV = 256
ITERS = 2
FEAT = 8192
FRAMES = 1024
N_FRAMES = 4
N_FEAT = 8


def scaled_field(key, height, breadth, amplitude):
    row_key, col_key, base_key = jax.random.split(key, 3)
    row_level = jax.random.uniform(row_key, (height, 1), jnp.float32)
    rise_share = 0.5
    base = jnp.clip(jax.random.normal(base_key, (height, breadth), jnp.float32), -3.0, 3.0)
    position = jnp.arange(breadth, dtype=jnp.float32)[None, :] / breadth
    col_level = (1.0 - rise_share) * jax.random.uniform(col_key, (1, breadth), jnp.float32) + rise_share * position
    return amplitude * base * jnp.power(10.0, row_level) * jnp.power(10.0, col_level) / 21.5


def draw_weights(key, part):
    return scaled_field(jax.random.fold_in(key, 11), C, FEAT, 0.1)


def draw_scaled_duals(key, part):
    return scaled_field(jax.random.fold_in(key, 23), C, FRAMES, 0.5)


def draw_acoustic(key, part):
    coord_key, sign_key, noise_key = jax.random.split(jax.random.fold_in(key, 37), 3)
    coords = jax.random.uniform(coord_key, (FRAMES, 2), jnp.float32, minval=-3.0, maxval=3.0)
    signs = jnp.where(jax.random.uniform(sign_key, (2, DIN), jnp.float32) < 0.5, -1.0, 1.0)
    noise = 0.2 * jnp.clip(jax.random.normal(noise_key, (FRAMES, DIN), jnp.float32), -3.0, 3.0)
    smooth = coords[:, 0:1] * signs[0:1, :] + coords[:, 1:2] * signs[1:2, :]
    return jnp.clip(smooth + noise, -6.0, 6.0)


def touch_ends(drawn, rng, smallest, largest):
    longest = drawn.shape.index(max(drawn.shape))
    spots = []
    for shift in (0, 1):
        where = [jax.random.randint(jax.random.fold_in(rng, axis), (), 0, length) for axis, length in enumerate(drawn.shape)]
        where[longest] = (where[longest] + shift) % drawn.shape[longest]
        spots.append(tuple(where))
    return drawn.at[spots[0]].set(smallest).at[spots[1]].set(largest)


def shard_levels(rng, shape, cuts, low, top_value):
    def one(dim, blocks):
        draws = jax.random.uniform(jax.random.fold_in(jax.random.fold_in(rng, 6), dim), (blocks,), jnp.float32, low / len(cuts), top_value / len(cuts))
        return jnp.repeat(jnp.exp(draws), shape[dim] // blocks).reshape((-1,) + (1,) * (len(shape) - dim - 1))

    loudness = one(*cuts[0])
    for cut in cuts[1:]:
        loudness = loudness * one(*cut)
    return loudness


def bell_draw(own_key, dims, width, reach, cuts=(), kind=jnp.bfloat16):
    loudness = shard_levels(own_key, dims, cuts, -0.22, 0.18) if cuts else 1.0
    array = jax.random.normal(own_key, dims, jnp.float32) * width * loudness
    return jnp.minimum(jnp.maximum(array, -reach), reach).astype(kind)


def setup_inputs(seed: int = 0) -> dict:
    splits = jax.random.split(jax.random.key(seed), 7)
    return {
        "acoustic": draw_acoustic(jax.random.fold_in(splits[6], 71), 0),
        "projection": bell_draw(splits[1], (DIN, FEAT), DIN ** -0.5, 0.25, ((1, 8),), jnp.float32),
        "phases": jnp.clip(jax.random.uniform(splits[2], (FEAT,), jnp.float32, -3.140625, 3.140625), -3.140625, 3.140625),
        "labels": touch_ends(jax.random.randint(splits[3], (FRAMES,), 0, C), jax.random.fold_in(splits[3], 1), 0, C - 1).astype(jnp.int32),
        "weights": draw_weights(jax.random.fold_in(splits[6], 71), 0),
        "scaled_duals": draw_scaled_duals(jax.random.fold_in(splits[6], 71), 0),
    }


highest = lax.Precision.HIGHEST
epsilon = 1e-06
ridge_weight = 2.0

def cosine_features(acoustic, projection, phases):
    mixed = jnp.dot(acoustic.astype(jnp.float32), projection.astype(jnp.float32), precision=highest, preferred_element_type=jnp.float32) + phases[None, :]
    return jnp.sqrt(2.0 / FEAT) * jnp.cos(mixed)

def ridge_solve(factor, right):
    middle = lax.linalg.triangular_solve(factor, right, left_side=False, lower=True, transpose_a=True)
    return lax.linalg.triangular_solve(factor, middle, left_side=False, lower=True, transpose_a=False)

def proximal(predicted, duals, target, penalty):
    shifted = predicted + duals
    inner = (2.0 * target + penalty * shifted) / (2.0 + penalty)
    split = jnp.where(target * shifted < 1.0, inner, shifted)
    miss = predicted - split
    duals_next = duals + miss
    residual = split - duals_next - predicted
    return (miss, duals_next, residual)

def reference(acoustic, projection, phases, labels, weights, scaled_duals):
    ridge = FR_DEV / FEAT
    group_rows = acoustic.reshape(N_FRAMES, FR_DEV, DIN)
    proj_blocks = projection.reshape(DIN, N_FEAT, FB).transpose(1, 0, 2)
    phase_blocks = phases.reshape(N_FEAT, FB)

    def factor_group(frame_block):

        def factor_block(pieces):
            basis = cosine_features(frame_block, pieces[0], pieces[1])
            inner = ridge * jnp.eye(FR_DEV, dtype=basis.dtype) + lax.dot_general(basis, basis, (((1,), (1,)), ((), ())), precision=highest)
            return jnp.linalg.cholesky(inner)
        return lax.map(factor_block, (proj_blocks, phase_blocks))
    factors = lax.map(factor_group, group_rows)
    label_groups = labels.reshape(N_FRAMES, FR_DEV)
    classes = jnp.arange(C, dtype=jnp.int32)
    target = jnp.where(classes[None, :, None] == label_groups[:, None, :], 1.0, -1.0).astype(weights.dtype)
    duals = scaled_duals.reshape(C, N_FRAMES, FR_DEV).transpose(1, 0, 2)
    blocks = weights.reshape(C, N_FEAT, FB).transpose(1, 0, 2)
    penalty = jnp.ones((), weights.dtype)
    for iteration in range(ITERS):

        def predict_group(frame_block):

            def add_block(total, pieces):
                basis = cosine_features(frame_block, pieces[0], pieces[1])
                return (total + lax.dot_general(pieces[2], basis, (((1,), (1,)), ((), ())), precision=highest), None)
            total, unused = lax.scan(add_block, jnp.zeros((C, FR_DEV), weights.dtype), (proj_blocks, phase_blocks, blocks))
            return total
        predicted = lax.map(predict_group, group_rows)
        miss, duals, residual = proximal(predicted, duals, target, penalty)
        primal = jnp.sum(miss * miss)

        def correct_group(total, pieces):
            frame_block, resid_group, factor_group_blocks = pieces

            def one_block(inner):
                basis = cosine_features(frame_block, inner[0], inner[1])
                proj = jnp.dot(resid_group.astype(jnp.float32), basis.astype(jnp.float32), precision=highest, preferred_element_type=jnp.float32) / N_FEAT
                coef = lax.dot_general(proj, basis, (((1,), (1,)), ((), ())), precision=highest)
                solved = ridge_solve(inner[3], coef)
                back = jnp.dot(solved.astype(jnp.float32), basis.astype(jnp.float32), precision=highest, preferred_element_type=jnp.float32)
                return inner[2] + (proj - back) / ridge
            return (total + lax.map(one_block, (proj_blocks, phase_blocks, blocks, factor_group_blocks)), None)
        summed, unused = lax.scan(correct_group, jnp.zeros_like(blocks), (group_rows, residual, factors))
        updated = penalty / (ridge_weight + penalty * N_FRAMES) * summed
        moved = updated - blocks
        change = jnp.sum(moved * moved)
        ratio = (primal / (FRAMES * C) + epsilon) / (N_FRAMES * penalty * penalty * change / (FEAT * C) + epsilon)
        next_penalty = penalty * jnp.sqrt(jnp.sqrt(ratio))
        duals = duals * (penalty / next_penalty)
        penalty = next_penalty
        blocks = updated
    return (blocks.transpose(1, 0, 2).reshape(C, FEAT), duals.transpose(1, 0, 2).reshape(C, FRAMES), penalty)
```

```python
import math
from functools import partial

import jax
import jax.numpy as jnp
from jax import lax
from jax.experimental import pallas as pl
from jax.experimental.pallas import tpu as pltpu
from jax.sharding import PartitionSpec as P

ITERS = 2

highest = lax.Precision.HIGHEST
f32 = jnp.float32
bf16 = jnp.bfloat16
epsilon = 1e-06
ridge_weight = 2.0
LANES = 128

TAU_A = 6.283203125
TAU_B = -1.7818063497543335e-05
TAU_C = 2.0 * math.pi - TAU_A - TAU_B
SINE = (
    0.9999999998894471,
    -0.16666666541091912,
    0.008333329256170866,
    -0.000198407020576212,
    2.751882149737428e-06,
    -2.3794188064307775e-08,
)


def sizes(class_count):
    return (class_count + 1 + 7) // 8 * 8


def exact_dot(a, b, contract=((1,), (0,))):
    return lax.dot_general(a, b, (contract, ((), ())), precision=highest, preferred_element_type=f32)


def halves(x):
    top = x.astype(bf16)
    return top, (x - top.astype(f32)).astype(bf16)


def quick_dot(a, b):
    a_top, a_low = halves(a)
    b_top, b_low = halves(b)
    return jnp.dot(
        jnp.concatenate([a_top, a_low, a_top], axis=1),
        jnp.concatenate([b_top, b_top, b_low], axis=0),
        preferred_element_type=f32,
    )


def scaled_cosine(x, scale):
    turns = jnp.round(x * (0.5 / math.pi))
    half = (((x - turns * TAU_A) - turns * TAU_B) - turns * TAU_C) * 0.5
    square = half * half
    value = SINE[-1]
    for term in SINE[-2::-1]:
        value = value * square + term
    sine = value * half
    return scale - (2.0 * scale) * (sine * sine)


def call(body, outs, args, name):
    return pl.pallas_call(
        body,
        out_shape=[jax.ShapeDtypeStruct(shape, f32) for shape in outs],
        name=name,
    )(*args)


def put_rows(ref, top, row):
    count = top.shape[0]
    ref[:count, :] = top
    ref[count : count + 1, :] = jnp.broadcast_to(row, (1, ref.shape[1]))
    rest = ref.shape[0] - count - 1
    if rest:
        ref[count + 1 :, :] = jnp.zeros((rest, ref.shape[1]), f32)


def total(x):
    return jnp.sum(jnp.sum(x, axis=0, keepdims=True), axis=1, keepdims=True)


def basis_body(scale, acoustic, projection, phases, basis):
    mixed = exact_dot(acoustic[...], projection[...]) + phases[...]
    basis[...] = scaled_cosine(mixed, scale)


def first_body(scale, acoustic, projection, phases, weights, basis, predicted):
    basis_body(scale, acoustic, projection, phases, basis)
    put_rows(predicted, exact_dot(weights[...], basis[...], ((1,), (1,))), jnp.zeros((1, 1), f32))


def inverse_body(ridge, rough, basis, inverse):
    count = basis.shape[0]
    gram = exact_dot(basis[...], basis[...], ((1,), (1,)))
    rows = lax.broadcasted_iota(jnp.int32, (count, count), 0)
    diagonal = rows == lax.broadcasted_iota(jnp.int32, (count, count), 1)
    matrix = gram + jnp.where(diagonal, ridge, 0.0)
    twice = jnp.where(diagonal, 2.0, 0.0)
    top = ridge + 1.0001 * jnp.sqrt(total(gram * gram))
    first = 2.0 / (ridge + top)
    spread = (top - ridge) / (top + ridge)

    def rescale(spread):
        square = spread * spread
        return 2.0 / (2.0 - square), square / (2.0 - square)

    scale, spread = rescale(spread)
    guess = (scale * first) * (twice - first * matrix)
    for step in range(rough + 2):
        dot = quick_dot if step < rough else exact_dot
        scale, spread = rescale(spread)
        guess = scale * dot(guess, twice - dot(matrix, guess))
    inverse[...] = guess


def proximal(predicted, duals, labels, penalty):
    classes = lax.broadcasted_iota(jnp.int32, predicted.shape, 0)
    target = jnp.where(classes == labels, 1.0, -1.0)
    shifted = predicted + duals
    inner = (2.0 * target + penalty * shifted) / (2.0 + penalty)
    split = jnp.where(target * shifted < 1.0, inner, shifted)
    miss = predicted - split
    duals_next = duals + miss
    return miss, duals_next, split - duals_next - predicted


def next_penalty(penalty, primal, change, primal_count, change_count, groups):
    ratio = (primal / primal_count + epsilon) / (groups * penalty * penalty * change / change_count + epsilon)
    return penalty * jnp.sqrt(jnp.sqrt(ratio))


def residual_body(blocks, counts, first, *refs):
    here, there, duals_in, labels, inverse = refs[:5]
    class_count = duals_in.shape[0]
    predicted = here[:class_count, :] + there[:class_count, :]
    duals = duals_in[...]
    if first:
        penalty = jnp.ones((1, 1), f32)
        solved, duals_out, penalty_out = refs[5:]
    else:
        primal, before, solved, duals_out, penalty_out = refs[5:]
        change = here[class_count : class_count + 1, :1] + there[class_count : class_count + 1, :1]
        before = before[:, :1]
        penalty = next_penalty(before, primal[:, :1], change, *counts)
        duals = duals * (before / penalty)
    miss, duals_next, residual = proximal(predicted, duals, labels[...], penalty)
    duals_out[...] = duals_next
    penalty_out[...] = jnp.broadcast_to(penalty, penalty_out.shape)
    put_rows(solved, exact_dot(residual * (1.0 / blocks), inverse[...]), total(miss * miss))


def tree(terms):
    while len(terms) > 1:
        terms = [terms[i] + terms[i + 1] for i in range(0, len(terms), 2)]
    return terms[0]


def spread_body(class_count, *refs):
    count = (len(refs) - 1) // 2
    solved, bases, out = refs[:count], refs[count:-1], refs[-1]
    primal = tree([s[class_count : class_count + 1, :1] for s in solved])
    put_rows(out, tree([exact_dot(s[:class_count, :], b[...]) for s, b in zip(solved, bases)]), primal)


def update_body(groups, last, here, there, weights, penalty, *refs):
    class_count = weights.shape[0]
    penalty = penalty[:, :1]
    old = weights[...]
    spread = here[:class_count, :] + there[:class_count, :]
    new = penalty / (ridge_weight + penalty * groups) * (groups * old + spread)
    moved = new - old
    change = total(moved * moved)
    if last:
        updated, primal_out, change_out = refs
        change_out[...] = jnp.broadcast_to(change, change_out.shape)
    else:
        basis, updated, primal_out, predicted = refs
        put_rows(predicted, exact_dot(new, basis[...], ((1,), (1,))), change)
    updated[...] = new
    row = slice(class_count, class_count + 1)
    primal_out[...] = here[row, :LANES] + there[row, :LANES]


def flip(x, axis, bit):
    return lax.ppermute(x, axis, [(i, i ^ bit) for i in range(lax.axis_size(axis))])


def bits_of(count, low=1):
    out = []
    while low < count:
        out.append(low)
        low *= 2
    return out


def shards(acoustic, projection, phases, labels, weights, scaled_duals):
    frames_here = acoustic.shape[0]
    width = projection.shape[1]
    class_count = weights.shape[0]
    blocks = lax.axis_size("feat")
    groups = lax.axis_size("frames")
    total_features = width * blocks
    total_frames = frames_here * groups
    ridge = frames_here / total_features
    scale = math.sqrt(2.0 / total_features)
    share = frames_here // blocks
    offset = lax.axis_index("feat") * share
    rows = sizes(class_count)
    counts = (total_frames * class_count, total_features * class_count, groups)
    phases = phases[None, :]
    labels = labels[None, :]
    feat_bits = bits_of(blocks)
    x_bits = bits_of(groups, 2)
    core_bit = groups > 1

    def over_feat(value):
        for bit in feat_bits[:-1]:
            value = value + flip(value, "feat", bit)
        return value, flip(value, "feat", feat_bits[-1])

    def over_x(value):
        held = [value]
        for bit in x_bits:
            held = held + [flip(v, "frames", bit) for v in held]
        return held

    basis, predicted = call(
        partial(first_body, scale),
        [(frames_here, width), (rows, frames_here)],
        (acoustic, projection, phases, weights),
        "first",
    )
    pair = over_feat(predicted)
    near = over_x(acoustic)[1:]
    bases = [basis] + [
        call(partial(basis_body, scale), [(frames_here, width)], (a, projection, phases), "basis")[0] for a in near
    ]
    (inverse,) = call(partial(inverse_body, ridge, 6), [(frames_here, frames_here)], (basis,), "inverse")
    duals, penalty, primal = scaled_duals, None, None
    for iteration in range(ITERS):
        last = iteration == ITERS - 1
        extra = () if iteration == 0 else (primal, penalty)
        solved, duals, penalty = call(
            partial(residual_body, blocks, counts, iteration == 0),
            [(rows, frames_here), (class_count, frames_here), (1, LANES)],
            (*pair, duals, labels, inverse, *extra),
            "residual",
        )
        (spread,) = call(
            partial(spread_body, class_count),
            [(rows, width)],
            (*over_x(solved), *bases),
            "spread",
        )
        outs = [(class_count, width), (1, LANES), (1, LANES) if last else (rows, frames_here)]
        args = (spread, flip(spread, "frames", 1), weights, penalty)
        weights, primal, third = call(
            partial(update_body, groups, last), outs, args if last else (*args, basis), "update"
        )
        if not last:
            pair = over_feat(third)
    duals = lax.dynamic_slice_in_dim(duals, offset, share, 1)
    change = lax.all_to_all(jnp.broadcast_to(third, (blocks, 8, LANES)), "feat", 0, 0)
    change = jnp.sum(change[:, 0, 0])
    before = penalty[0, 0]
    penalty = next_penalty(before, primal[0, 0], change, *counts)
    return weights, duals * (before / penalty), penalty


def solution(mesh):
    return jax.shard_map(
        shards,
        mesh=mesh,
        in_specs=(
            P("frames", None),
            P(None, "feat"),
            P("feat"),
            P("frames"),
            P(None, "feat"),
            P(None, "frames"),
        ),
        out_specs=(P(None, "feat"), P(None, ("frames", "feat")), P()),
        check_vma=False,
    )
```
